128 devices in a mesh: walk: 4 (over y_hi, core), stretch: 32 (over z, y_lo, x).
Axes of the slice: x: 4, y: 4 (y_hi: 2, y_lo: 2; y = y_hi * 2 + y_lo), z: 4, core: 2. Of those that a mesh axis runs over, the one named last changes fastest.
Arguments:
- walkers: float32 [256, 48, 512], P(('walk', 'stretch')), may hold values from -6 to 6
- inverse_intersection: float32 [256, 48, 48], P(('walk', 'stretch')), may hold values from -0.875 to 0.875
- half_rotated: bfloat16 [1024, 48, 512], P('stretch'), may hold values from -0.076546554 to 0.076546554
- cholesky: bfloat16 [1024, 512, 512], P('stretch'), may hold values from -0.015625 to 0.015625
- field_noise: float32 [256, 1024], P('walk', 'stretch'), may hold values from -6 to 6
- branch_sources: int32 [256], P(('walk', 'stretch')), may hold values from 0 to 255, as said below
Outputs:
- force_bias: float32 [256, 1024], P('walk', 'stretch')
- exchange_energy: float32 [256], P(('walk', 'stretch'))
- new_walkers: float32 [256, 48, 512], P(('walk', 'stretch'))
The draws below stay inside these ranges and needn't reach their ends.
Inputs may be any that keep to these rules, and one draw needn't show every extreme that they name: `branch_sources`: walker d lies in column (d // 2) % 32; every entry names a walker of the same column as its destination slot. A walker may be named by several slots or by none.
All inputs are finite; a program needn't handle non-finite values.
Results may differ from the reference program's by a relative error of at most 0.0029.
Values may be sent and summed in bfloat16 or wider, within the bound.
No kernel may reach another device: no remote copies, remote signals or barrier semaphores. Data moves between devices by JAX's collectives and lax.ppermute only.
A program may use at most 256 MiB of HBM per device.

```python
import math
import jax
import jax.numpy as jnp
from jax import lax

M = 512
NOCC = 48
NCHOL = 1024
WD = 2
ORDERS = 2
GROUP_WALKERS = 64
WALKERS = 256


def draw_half_rotated(key, part):
    ramp = 1.0 + 2.0 * jnp.arange(NCHOL, dtype=jnp.float32) / NCHOL
    base = jax.random.truncated_normal(key, -4.0, 4.0, (NCHOL, NOCC, M), jnp.float32)
    values = base * ramp[:, None, None] / math.sqrt(NOCC * M)
    return values.astype(jnp.bfloat16)


def draw_branch_sources(key, part):
    first, second, third = jax.random.split(jax.random.fold_in(key, 7), 3)
    walk_count = WALKERS // GROUP_WALKERS
    destination = jnp.arange(WALKERS, dtype=jnp.int32)
    column = destination // WD % (GROUP_WALKERS // WD)
    walk_one = jax.random.randint(first, (WALKERS,), 0, walk_count, dtype=jnp.int32)
    walk_two = jax.random.randint(second, (WALKERS,), 0, walk_count, dtype=jnp.int32)
    local_row = jax.random.randint(third, (WALKERS,), 0, WD, dtype=jnp.int32)
    source = jnp.minimum(walk_one, walk_two) * GROUP_WALKERS + column * WD + local_row
    source = source.at[0].set(0).at[WALKERS - 1].set(WALKERS - 1)
    return source.astype(jnp.int32)


def levels(stream_key, dims, cuts, smallest, top_value):
    level, own = 1.0, jax.random.fold_in(stream_key, 6)
    for dim, parts in cuts:
        heights = jnp.exp(jax.random.uniform(jax.random.fold_in(own, dim), (parts,), jnp.float32, smallest / len(cuts), top_value / len(cuts)))
        level = level * jnp.repeat(heights, dims[dim] // parts).reshape([-1 if axis == dim else 1 for axis in range(len(dims))])
    return level


def scatter_about(key, shape, scale, limit, shards=(), held_as=jnp.bfloat16):
    level = levels(key, shape, shards, -0.22, 0.18) if shards else 1.0
    entries = jax.random.normal(key, shape, jnp.float32) * scale * level
    return jnp.minimum(jnp.maximum(entries, -limit), limit).astype(held_as)


def setup_inputs(seed: int = 0) -> dict:
    key_of = jax.random.split(jax.random.key(seed), 7)
    walkers = scatter_about(key_of[0], (WALKERS, NOCC, M), 1.0, 6.0, ((0, 128),), jnp.float32)
    inverse_intersection = scatter_about(key_of[1], (WALKERS, NOCC, NOCC), NOCC ** -0.5, 0.875, ((0, 128),), jnp.float32)
    half_rotated = draw_half_rotated(jax.random.fold_in(key_of[6], 71), 0)
    cholesky = scatter_about(key_of[3], (NCHOL, M, M), (2.0 / (M * NCHOL) ** 0.5), 0.015625, ((0, 32),))
    field_noise = scatter_about(key_of[4], (WALKERS, NCHOL), 1.0, 6.0, ((0, 4), (1, 32)), jnp.float32)
    branch_sources = draw_branch_sources(jax.random.fold_in(key_of[6], 71), 0)
    return dict(walkers=walkers, inverse_intersection=inverse_intersection, half_rotated=half_rotated, cholesky=cholesky, field_noise=field_noise, branch_sources=branch_sources)


def reference(walkers, inverse_intersection, half_rotated, cholesky, field_noise, branch_sources):
    green = jnp.einsum("wij,wjp->wip", inverse_intersection, walkers, precision=lax.Precision.HIGHEST).astype(jnp.bfloat16)
    hr_flat = half_rotated.reshape(NCHOL * NOCC, M)
    step_rows = math.gcd(WALKERS, 4)

    def contract(green_block):
        intersections = lax.dot_general(hr_flat, green_block.reshape(step_rows * NOCC, M), (((1,), (1,)), ((), ())), preferred_element_type=jnp.float32)
        intersections = intersections.reshape(NCHOL, NOCC, step_rows, NOCC)
        bias_block = 2.0 * jnp.trace(intersections, axis1=1, axis2=3).T
        energy_block = -0.5 * jnp.sum(intersections * jnp.transpose(intersections, (0, 3, 2, 1)), axis=(0, 1, 3))
        return bias_block, energy_block

    bias_blocks, energy_blocks = lax.map(contract, green.reshape(WALKERS // step_rows, step_rows, NOCC, M))
    force_bias = bias_blocks.reshape(WALKERS, NCHOL)
    exchange_energy = energy_blocks.reshape(WALKERS)
    fields = (0.05 * (field_noise - force_bias)).astype(jnp.bfloat16)
    chol_flat = cholesky.reshape(NCHOL, M * M)
    block_size = math.gcd(WALKERS, 16)

    def one_block(operands):
        psi_block, field_block = operands
        matrix = jnp.dot(field_block, chol_flat, preferred_element_type=jnp.float32).reshape(block_size, M, M)
        return jnp.einsum("bip,bpq->biq", psi_block.astype(jnp.float32), matrix, precision=lax.Precision.HIGHEST)

    term = walkers
    propagated = walkers
    for degree in range(1, ORDERS + 1):
        rows_now = term.astype(jnp.bfloat16)
        summed = lax.map(one_block, (rows_now.reshape(WALKERS // block_size, block_size, NOCC, M), fields.reshape(WALKERS // block_size, block_size, NCHOL)))
        term = summed.reshape(WALKERS, NOCC, M) / degree
        propagated = propagated + term
    new_walkers = jnp.take(propagated, branch_sources, axis=0)
    return force_bias, exchange_energy, new_walkers
```

```python
import functools

import jax
import jax.numpy as jnp
import numpy as np
from jax import lax
from jax.experimental import pallas as pl
from jax.experimental.pallas import tpu as pltpu
from jax.sharding import PartitionSpec as P

ORDERS = 2
Z, Y, X = 4, 2, 4
S = Z * Y * X
STEP = {"z": (1, 0, 0), "y": (0, 1, 0), "x": (0, 0, 1)}
HEARD = (0, -1, 1, -2)
ORDER_A = "yxz"
ORDER_B = "yzx"
PAD = 64
WB = 8
F32 = jnp.float32
BF16 = jnp.bfloat16


def encode(z, y, x):
    return (z % Z) * (Y * X) + (y % Y) * X + (x % X)


def decode(s):
    return s // (Y * X), s // X % Y, s % X


def shift(a, axis, k):
    d = STEP[axis]
    pairs = []
    for s in range(S):
        z, y, x = decode(s)
        pairs.append((s, encode(z + d[0] * k, y + d[1] * k, x + d[2] * k)))
    return lax.ppermute(a, "stretch", pairs)


def gather_staged(a, order):
    for axis in order:
        if axis == "y":
            a = jnp.concatenate([a, shift(a, axis, 1)], 0)
        else:
            a = jnp.concatenate([a, shift(a, axis, 1), shift(a, axis, -1), shift(a, axis, 2)], 0)
    return a


def slots(order):
    table = np.zeros((S, S), np.int32)
    for s in range(S):
        offsets = [(0, 0, 0)]
        for axis in order:
            d = STEP[axis]
            heard = HEARD[:2] if axis == "y" else HEARD
            offsets = [tuple(o[i] + d[i] * h for i in range(3)) for h in heard for o in offsets]
        z, y, x = decode(s)
        for slot, o in enumerate(offsets):
            table[s, encode(z + o[0], y + o[1], x + o[2])] = slot
    return table


def gather_walkers(a):
    return gather_staged(a[0:1], ORDER_A), gather_staged(a[1:2], ORDER_B)


def intersect_kernel(slot_ref, ga_ref, gb_ref, he_ref, ho_ref, ht_ref, hts_ref, e_ref, s_ref, gp, gps, ge, go):
    @pl.when(pl.program_id(0) == 0)
    def _():
        gp[...] = jnp.zeros_like(gp)
        gps[...] = jnp.zeros_like(gps)

    nocc = ga_ref.shape[1]
    base = pl.program_id(0) * (WB // 2)
    for k in range(WB // 2):
        a = ga_ref[slot_ref[0, base + k]]
        b = gb_ref[slot_ref[1, base + k]]
        gp[2 * k * PAD : 2 * k * PAD + nocc, :] = a
        gp[(2 * k + 1) * PAD : (2 * k + 1) * PAD + nocc, :] = b
        gps[(2 * k + 1) * PAD : (2 * k + 1) * PAD + nocc, :] = a
        gps[2 * k * PAD : 2 * k * PAD + nocc, :] = b
        ge[k * nocc : (k + 1) * nocc, :] = a
        go[k * nocc : (k + 1) * nocc, :] = b
    nt = (((1,), (1,)), ((), ()))
    ae = lax.dot_general(he_ref[...], gp[...], nt, preferred_element_type=F32)
    ao = lax.dot_general(ho_ref[...], gps[...], nt, preferred_element_type=F32)
    be = jnp.dot(ge[...], ht_ref[...], preferred_element_type=F32)
    bo = jnp.dot(go[...], hts_ref[...], preferred_element_type=F32)
    lane = lax.broadcasted_iota(jnp.int32, (8, 128), 1)
    row = lax.broadcasted_iota(jnp.int32, (8, 128), 0)
    low = lane < PAD
    group = lane % PAD // 8
    diagonal = (lane % 8 == row) & (lane % PAD < nocc)
    tiles = nocc // 8
    g_pairs = he_ref.shape[0] // nocc
    for k in range(WB // 2):
        acc_e = jnp.zeros((8, 128), F32)
        acc_o = jnp.zeros((8, 128), F32)
        for g in range(g_pairs):
            de = do = None
            for t in range(tiles):
                rg = slice(g * nocc + t * 8, g * nocc + t * 8 + 8)
                rw = slice(k * nocc + t * 8, k * nocc + t * 8 + 8)
                lw = slice(k * 128, k * 128 + 128)
                lg = slice(g * 128, g * 128 + 128)
                a0, a1 = ae[rg, lw], ao[rg, lw]
                c0, c1 = be[rw, lg], bo[rw, lg]
                acc_e += a0 * jnp.where(low, c0, c1)
                acc_o += a1 * jnp.where(low, c1, c0)
                de = a0 if t == 0 else jnp.where(group == t, a0, de)
                do = a1 if t == 0 else jnp.where(group == t, a1, do)
            s_ref[k, 0, g : g + 1, :] = jnp.sum(jnp.where(diagonal, de, 0.0), axis=0, keepdims=True)
            s_ref[k, 1, g : g + 1, :] = jnp.sum(jnp.where(diagonal, do, 0.0), axis=0, keepdims=True)
        e_ref[k, 0] = acc_e
        e_ref[k, 1] = acc_o


def intersect(table, ga, gb, half_rotated):
    vectors, nocc, m = half_rotated.shape
    walkers = 2 * ga.shape[0]
    he = half_rotated[0::2].reshape(vectors // 2 * nocc, m)
    ho = half_rotated[1::2].reshape(vectors // 2 * nocc, m)
    padded = jnp.pad(half_rotated, ((0, 0), (0, PAD - nocc), (0, 0)))
    swapped = padded.reshape(vectors // 2, 2, PAD, m)[:, ::-1]
    ht = padded.reshape(vectors * PAD, m).T
    hts = swapped.reshape(vectors * PAD, m).T
    steps = walkers // WB
    vmem = pl.BlockSpec(memory_space=pltpu.VMEM)
    sums, diag = pl.pallas_call(
        intersect_kernel,
        grid=(steps,),
        in_specs=[pl.BlockSpec(memory_space=pltpu.SMEM)] + [vmem] * 6,
        out_specs=[
            pl.BlockSpec((WB // 2, 2, 8, 128), lambda i: (i, 0, 0, 0)),
            pl.BlockSpec((WB // 2, 2, vectors // 2, 128), lambda i: (i, 0, 0, 0)),
        ],
        out_shape=[
            jax.ShapeDtypeStruct((walkers // 2, 2, 8, 128), F32),
            jax.ShapeDtypeStruct((walkers // 2, 2, vectors // 2, 128), F32),
        ],
        scratch_shapes=[
            pltpu.VMEM((WB * PAD, m), BF16),
            pltpu.VMEM((WB * PAD, m), BF16),
            pltpu.VMEM((WB // 2 * nocc, m), BF16),
            pltpu.VMEM((WB // 2 * nocc, m), BF16),
        ],
        compiler_params=pltpu.CompilerParams(vmem_limit_bytes=60 << 20),
        cost_estimate=pl.CostEstimate(
            flops=4 * vectors * nocc * walkers * PAD * m, bytes_accessed=16 << 20, transcendentals=0
        ),
        name="intersect",
    )(table, ga, gb, he, ho, ht, hts)
    halves = jnp.sum(diag.reshape(walkers // 2, 2, vectors // 2, 2, PAD), -1)
    even, odd = halves[:, 0], halves[:, 1, :, ::-1]
    bias = 2.0 * jnp.stack([even, odd], 2)
    bias = jnp.transpose(bias, (0, 3, 1, 2)).reshape(walkers, vectors)
    parts = jnp.sum(sums.reshape(walkers // 2, 2, 8, 2, PAD), (2, 4))
    energy = -0.5 * (parts[:, 0] + parts[:, 1, ::-1]).reshape(walkers)
    return bias, energy


def field_kernel(slot_ref, f_ref, pa_ref, pb_ref, c_ref, h_ref, o_ref, fbd, hold):
    step = pl.program_id(0)
    walkers, vectors = f_ref.shape
    m = c_ref.shape[2]

    @pl.when(step == 0)
    def _():
        rows, cols = walkers * 8, vectors * 8
        r = lax.broadcasted_iota(jnp.int32, (rows, walkers), 0) // 8
        w = lax.broadcasted_iota(jnp.int32, (rows, walkers), 1)
        pick_w = jnp.where(r == w, 1.0, 0.0).astype(BF16)
        v = lax.broadcasted_iota(jnp.int32, (vectors, cols), 0)
        c = lax.broadcasted_iota(jnp.int32, (vectors, cols), 1) // 8
        pick_v = jnp.where(v == c, 1.0, 0.0).astype(BF16)
        spread = jnp.dot(pick_w, f_ref[...], preferred_element_type=F32).astype(BF16)
        spread = jnp.dot(spread, pick_v, preferred_element_type=F32)
        rr = lax.broadcasted_iota(jnp.int32, (rows, cols), 0) % 8
        cc = lax.broadcasted_iota(jnp.int32, (rows, cols), 1) % 8
        fbd[...] = jnp.where(rr == cc, spread, 0.0).astype(BF16)

    block = c_ref[...].astype(F32)
    lo = block[:, :8, :].reshape(vectors * 8, m).astype(BF16)
    hi = block[:, 8:, :].reshape(vectors * 8, m).astype(BF16)
    hlo = jnp.dot(fbd[...], lo, preferred_element_type=F32).reshape(walkers, 8, m)
    hhi = jnp.dot(fbd[...], hi, preferred_element_type=F32).reshape(walkers, 8, m)
    h = jnp.concatenate([hlo, hhi], axis=1).astype(BF16)
    h_ref[...] = h
    hold[:, pl.ds(pl.multiple_of(step * 16, 16), 16), :] = h

    @pl.when(step == pl.num_programs(0) - 1)
    def _():
        def one(i, carry):
            a = pa_ref[slot_ref[0, i]]
            b = pb_ref[slot_ref[1, i]]
            o_ref[2 * i] = jnp.dot(a, hold[2 * i], preferred_element_type=F32).astype(BF16)
            o_ref[2 * i + 1] = jnp.dot(b, hold[2 * i + 1], preferred_element_type=F32).astype(BF16)
            return carry

        lax.fori_loop(0, walkers // 2, one, 0)


def field_apply(table, fields, pa, pb, cholesky):
    walkers, vectors = fields.shape
    m = cholesky.shape[1]
    nocc = pa.shape[1]
    vmem = pl.BlockSpec(memory_space=pltpu.VMEM)
    return pl.pallas_call(
        field_kernel,
        grid=(m // 16,),
        in_specs=[
            pl.BlockSpec(memory_space=pltpu.SMEM),
            vmem,
            vmem,
            vmem,
            pl.BlockSpec((vectors, 16, m), lambda i: (0, i, 0)),
        ],
        out_specs=[pl.BlockSpec((walkers, 16, m), lambda i: (0, i, 0)), vmem],
        out_shape=[
            jax.ShapeDtypeStruct((walkers, m, m), BF16),
            jax.ShapeDtypeStruct((walkers, nocc, m), BF16),
        ],
        scratch_shapes=[pltpu.VMEM((walkers * 8, vectors * 8), BF16), pltpu.VMEM((walkers, m, m), BF16)],
        compiler_params=pltpu.CompilerParams(vmem_limit_bytes=60 << 20),
        cost_estimate=pl.CostEstimate(flops=12 << 30, bytes_accessed=64 << 20, transcendentals=0),
        name="field_apply",
    )(table, fields, pa, pb, cholesky)


def apply_kernel(slot_ref, pa_ref, pb_ref, h_ref, o_ref):
    pairs = h_ref.shape[0] // 2
    base = pl.program_id(0) * pairs
    for k in range(pairs):
        a = pa_ref[slot_ref[0, base + k]]
        b = pb_ref[slot_ref[1, base + k]]
        o_ref[2 * k] = jnp.dot(a, h_ref[2 * k], preferred_element_type=F32).astype(BF16)
        o_ref[2 * k + 1] = jnp.dot(b, h_ref[2 * k + 1], preferred_element_type=F32).astype(BF16)


def apply(table, pa, pb, h):
    walkers, m, _ = h.shape
    nocc = pa.shape[1]
    vmem = pl.BlockSpec(memory_space=pltpu.VMEM)
    block = 4
    return pl.pallas_call(
        apply_kernel,
        grid=(walkers // block,),
        in_specs=[
            pl.BlockSpec(memory_space=pltpu.SMEM),
            vmem,
            vmem,
            pl.BlockSpec((block, m, m), lambda i: (i, 0, 0)),
        ],
        out_specs=pl.BlockSpec((block, nocc, m), lambda i: (i, 0, 0)),
        out_shape=jax.ShapeDtypeStruct((walkers, nocc, m), BF16),
        compiler_params=pltpu.CompilerParams(vmem_limit_bytes=60 << 20),
        cost_estimate=pl.CostEstimate(flops=6 << 30, bytes_accessed=40 << 20, transcendentals=0),
        name="apply",
    )(table, pa, pb, h)


def scatter_sum(part):
    walkers, nocc, m = part.shape
    got = lax.all_to_all(part.reshape(S, walkers // S, nocc, m), "stretch", 0, 0, tiled=True)
    return jnp.sum(got.astype(F32), 0)


def shards(walkers, inverse_intersection, half_rotated, cholesky, field_noise, branch_sources):
    walker_count = walkers.shape[0]
    group_size = walker_count * S
    place = lax.axis_index("stretch")
    both = np.stack([slots(ORDER_A), slots(ORDER_B)], 1)
    table = lax.dynamic_index_in_dim(jnp.asarray(both), place, 0, keepdims=False)
    green = jnp.einsum(
        "wij,wjp->wip", inverse_intersection, walkers, precision=lax.Precision.HIGHEST
    ).astype(BF16)
    ga, gb = gather_walkers(green)
    pa, pb = gather_walkers(walkers.astype(BF16))
    force_bias, energy = intersect(table, ga, gb, half_rotated)
    fields = (0.05 * (field_noise - force_bias)).astype(BF16)
    h, part = field_apply(table, fields, pa, pb, cholesky)
    got = lax.all_to_all(energy.reshape(S, walker_count), "stretch", 0, 0, tiled=True)
    exchange_energy = jnp.sum(got, 0)
    first = scatter_sum(part)
    qa, qb = gather_walkers(first.astype(BF16))
    second = scatter_sum(apply(table, qa, qb, h)) / 2
    propagated = walkers + first + second
    column = lax.all_gather(propagated, "walk", axis=0, tiled=True)
    position = branch_sources // group_size * walker_count + branch_sources % walker_count
    picked = jnp.take(column, position, axis=0)
    return (force_bias, exchange_energy, picked)


def solution(mesh):
    placed = (
        P(("walk", "stretch"), None, None),
        P(("walk", "stretch"), None, None),
        P("stretch", None, None),
        P("stretch", None, None),
        P("walk", "stretch"),
        P(("walk", "stretch")),
    )
    return jax.shard_map(
        shards,
        mesh=mesh,
        in_specs=placed,
        out_specs=(
            P("walk", "stretch"),
            P(("walk", "stretch")),
            P(("walk", "stretch"), None, None),
        ),
        check_vma=False,
    )
```

```python
import functools

import jax
import jax.numpy as jnp
import numpy as np
from jax import lax
from jax.experimental import pallas as pl
from jax.experimental.pallas import tpu as pltpu
from jax.sharding import PartitionSpec as P

ORDERS = 2
Z, Y, X = 4, 2, 4
S = Z * Y * X
STEP = {"z": (1, 0, 0), "y": (0, 1, 0), "x": (0, 0, 1)}
HEARD = (0, -1, 1, -2)
ORDER_A = "yxz"
ORDER_B = "yzx"
PAD = 64
WB = 8
F32 = jnp.float32
BF16 = jnp.bfloat16
NT = (((1,), (1,)), ((), ()))


def encode(z, y, x):
    return (z % Z) * (Y * X) + (y % Y) * X + (x % X)


def decode(s):
    return s // (Y * X), s // X % Y, s % X


def shift(a, axis, k):
    d = STEP[axis]
    pairs = []
    for s in range(S):
        z, y, x = decode(s)
        pairs.append((s, encode(z + d[0] * k, y + d[1] * k, x + d[2] * k)))
    return lax.ppermute(a, "stretch", pairs)


def around(a, axis):
    return [a, shift(a, axis, 1), shift(a, axis, -1), shift(a, axis, 2)]


def slots(order):
    table = np.zeros((S, S), np.int32)
    for s in range(S):
        offsets = [(0, 0, 0)]
        for axis in order:
            d = STEP[axis]
            heard = HEARD[:2] if axis == "y" else HEARD
            offsets = [tuple(o[i] + d[i] * h for i in range(3)) for h in heard for o in offsets]
        z, y, x = decode(s)
        for slot, o in enumerate(offsets):
            table[s, encode(z + o[0], y + o[1], x + o[2])] = slot
    return table


def gather_walkers(a):
    both = jnp.concatenate([a, shift(a, "y", 1)], 0)
    near = [jnp.concatenate(around(both[i::2], o[1]), 0) for i, o in enumerate((ORDER_A, ORDER_B))]
    far = [around(n, o[2]) for n, o in zip(near, (ORDER_A, ORDER_B))]
    return list(zip(*far))


def intersect_kernel(chunk, chunks, *refs):
    owner_ref, ga_ref, gb_ref, hr_ref = refs[:4]
    final = chunk == chunks - 1
    if final:
        n_ref, *earlier = refs[4 : 4 + chunks]
        b_ref, f_ref, e_ref, total = refs[4 + chunks : 8 + chunks]
    else:
        total = refs[4]
    he, ho, hp, hps, gp, gps, ge, go, sums = refs[-9:]
    step = pl.program_id(0)
    vectors, nocc = hr_ref.shape[:2]
    half = vectors // 2

    @pl.when(step == 0)
    def _():
        gp[...] = jnp.zeros_like(gp)
        gps[...] = jnp.zeros_like(gps)
        hp[...] = jnp.zeros_like(hp)
        hps[...] = jnp.zeros_like(hps)
        sums[...] = jnp.zeros_like(sums)
        total[...] = jnp.zeros_like(total)
        for g in range(half):
            for side, dense in ((0, he), (1, ho)):
                v = hr_ref[side * half + g]
                dense[g * nocc : (g + 1) * nocc, :] = v
                at = (2 * g + side) * PAD
                hp[at : at + nocc, :] = v
                at = (2 * g + 1 - side) * PAD
                hps[at : at + nocc, :] = v

    pairs = WB // 2
    for k in range(pairs):
        a = ga_ref[step * pairs + k, :nocc]
        b = gb_ref[step * pairs + k, :nocc]
        gp[2 * k * PAD : 2 * k * PAD + nocc, :] = a
        gp[(2 * k + 1) * PAD : (2 * k + 1) * PAD + nocc, :] = b
        gps[(2 * k + 1) * PAD : (2 * k + 1) * PAD + nocc, :] = a
        gps[2 * k * PAD : 2 * k * PAD + nocc, :] = b
        ge[k * nocc : (k + 1) * nocc, :] = a
        go[k * nocc : (k + 1) * nocc, :] = b
    ae = lax.dot_general(he[...], gp[...], NT, preferred_element_type=F32)
    ao = lax.dot_general(ho[...], gps[...], NT, preferred_element_type=F32)
    be = lax.dot_general(ge[...], hp[...], NT, preferred_element_type=F32)
    bo = lax.dot_general(go[...], hps[...], NT, preferred_element_type=F32)
    lane = lax.broadcasted_iota(jnp.int32, (8, 128), 1)
    row = lax.broadcasted_iota(jnp.int32, (8, 128), 0)
    low = lane < PAD
    group = lane % PAD // 8
    diagonal = (lane % 8 == row) & (lane % PAD < nocc)
    for k in range(pairs):
        acc_e = jnp.zeros((8, 128), F32)
        acc_o = jnp.zeros((8, 128), F32)
        lw = slice(k * 128, k * 128 + 128)
        for g in range(half):
            de = do = None
            for t in range(nocc // 8):
                rg = slice(g * nocc + t * 8, g * nocc + t * 8 + 8)
                rw = slice(k * nocc + t * 8, k * nocc + t * 8 + 8)
                lg = slice(g * 128, g * 128 + 128)
                a0, a1 = ae[rg, lw], ao[rg, lw]
                c0, c1 = be[rw, lg], bo[rw, lg]
                acc_e += a0 * jnp.where(low, c0, c1)
                acc_o += a1 * jnp.where(low, c1, c0)
                de = a0 if t == 0 else jnp.where(group == t, a0, de)
                do = a1 if t == 0 else jnp.where(group == t, a1, do)
            sums[0, g : g + 1, lw] = jnp.sum(jnp.where(diagonal, de, 0.0), axis=0, keepdims=True)
            sums[1, g : g + 1, lw] = jnp.sum(jnp.where(diagonal, do, 0.0), axis=0, keepdims=True)
        sums[0, half : half + 1, lw] = jnp.sum(acc_e, axis=0, keepdims=True)
        sums[1, half : half + 1, lw] = jnp.sum(acc_o, axis=0, keepdims=True)
    walkers = total.shape[2]
    side = lax.broadcasted_iota(jnp.int32, (128, walkers), 0) // PAD
    target = lax.broadcasted_iota(jnp.int32, (128, walkers), 1)
    base = chunk * ga_ref.shape[0] + step * pairs
    for parity in range(2):
        picks = []
        for k in range(pairs):
            wa, wb = 2 * owner_ref[0, base + k], 2 * owner_ref[1, base + k] + 1
            walker = jnp.where(side == parity, wa, wb)
            picks.append(jnp.where(walker == target, 1.0, 0.0))
        pick = jnp.concatenate(picks, axis=0).astype(BF16)
        whole = sums[parity]
        first = whole.astype(BF16)
        rest = whole - first.astype(F32)
        second = rest.astype(BF16)
        third = (rest - second.astype(F32)).astype(BF16)
        acc = jnp.dot(first, pick, preferred_element_type=F32)
        acc += jnp.dot(second, pick, preferred_element_type=F32)
        acc += jnp.dot(third, pick, preferred_element_type=F32)
        total[parity] += acc

    if final:

        @pl.when(step == pl.num_programs(0) - 1)
        def _():
            whole = total[...]
            for other in earlier:
                whole += other[...]
            bias = 2.0 * jnp.concatenate([whole[0, :half], whole[1, :half]], axis=0)
            b_ref[...] = bias
            f_ref[...] = (0.05 * (n_ref[...] - bias)).astype(BF16)
            e_ref[...] = -0.5 * (whole[0, half:] + whole[1, half:])


def intersect(owner, pieces, half_rotated, noise):
    vectors, nocc, m = half_rotated.shape
    chunks = len(pieces)
    held = pieces[0][0].shape[0]
    walkers = 2 * held * chunks
    vmem = pl.BlockSpec(memory_space=pltpu.VMEM)
    total = jax.ShapeDtypeStruct((2, vectors // 2 + 8, walkers), F32)
    earlier = []
    for chunk, (ga, gb) in enumerate(pieces):
        final = chunk == chunks - 1
        inputs = [owner, ga, gb, half_rotated] + ([noise.T] + earlier if final else [])
        outs = [total]
        if final:
            outs = [
                jax.ShapeDtypeStruct((vectors, walkers), F32),
                jax.ShapeDtypeStruct((vectors, walkers), BF16),
                jax.ShapeDtypeStruct((8, walkers), F32),
                total,
            ]
        got = pl.pallas_call(
            functools.partial(intersect_kernel, chunk, chunks),
            grid=(2 * held // WB,),
            in_specs=[pl.BlockSpec(memory_space=pltpu.SMEM)] + [vmem] * (len(inputs) - 1),
            out_specs=[vmem] * len(outs),
            out_shape=outs,
            scratch_shapes=[
                pltpu.VMEM((vectors // 2 * nocc, m), BF16),
                pltpu.VMEM((vectors // 2 * nocc, m), BF16),
                pltpu.VMEM((vectors * PAD, m), BF16),
                pltpu.VMEM((vectors * PAD, m), BF16),
                pltpu.VMEM((WB * PAD, m), BF16),
                pltpu.VMEM((WB * PAD, m), BF16),
                pltpu.VMEM((WB // 2 * nocc, m), BF16),
                pltpu.VMEM((WB // 2 * nocc, m), BF16),
                pltpu.VMEM((2, vectors // 2 + 8, WB // 2 * 128), F32),
            ],
            compiler_params=pltpu.CompilerParams(vmem_limit_bytes=36 << 20),
            cost_estimate=pl.CostEstimate(
                flops=4 * vectors * nocc * 2 * held * PAD * m, bytes_accessed=4 << 20, transcendentals=0
            ),
            name=f"intersect_{chunk}",
        )(*inputs)
        earlier.append(got[0])
    bias, fields, energy, _ = got
    return bias.T, fields, energy[0]


def field_kernel(owner_ref, f_ref, c_ref, *refs):
    *pieces, h_ref, o_ref, spread, hold, sems = refs
    step = pl.program_id(0)
    last = pl.num_programs(0) - 1
    vectors, walkers = f_ref.shape
    rows_p, m = c_ref.shape[1:]
    nocc = o_ref.shape[2]

    @pl.when(step == 0)
    def _():
        rows, cols = walkers * 8, vectors * 8
        r = lax.broadcasted_iota(jnp.int32, (rows, walkers), 0) // 8
        w = lax.broadcasted_iota(jnp.int32, (rows, walkers), 1)
        pick_w = jnp.where(r == w, 1.0, 0.0).astype(BF16)
        v = lax.broadcasted_iota(jnp.int32, (vectors, cols), 0)
        c = lax.broadcasted_iota(jnp.int32, (vectors, cols), 1) // 8
        pick_v = jnp.where(v == c, 1.0, 0.0).astype(BF16)
        wide = lax.dot_general(pick_w, f_ref[...], NT, preferred_element_type=F32).astype(BF16)
        wide = jnp.dot(wide, pick_v, preferred_element_type=F32)
        rr = lax.broadcasted_iota(jnp.int32, (rows, cols), 0) % 8
        cc = lax.broadcasted_iota(jnp.int32, (rows, cols), 1) % 8
        spread[...] = jnp.where(rr == cc, wide, 0.0).astype(BF16)

    for q in range(0, rows_p, 16):
        block = c_ref[:, q : q + 16, :].astype(F32)
        lo = block[:, :8, :].reshape(vectors * 8, m).astype(BF16)
        hi = block[:, 8:, :].reshape(vectors * 8, m).astype(BF16)
        hlo = jnp.dot(spread[...], lo, preferred_element_type=F32).reshape(walkers, 8, m)
        hhi = jnp.dot(spread[...], hi, preferred_element_type=F32).reshape(walkers, 8, m)
        at = pl.ds(pl.multiple_of(step * rows_p + q, 16), 16)
        hold[:, at, :] = jnp.concatenate([hlo, hhi], axis=1).astype(BF16)

    @pl.when(step == last)
    def _():
        blocks = sems.shape[0]
        size = walkers // blocks

        def keep(b):
            at = slice(b * size, (b + 1) * size)
            return pltpu.make_async_copy(hold.at[at], h_ref.at[at], sems.at[b])

        for b in range(blocks):
            keep(b).start()
        count = pieces[0].shape[0]
        for p, ref in enumerate(pieces):

            def one(i, carry, p=p, ref=ref):
                who = owner_ref[p % 2, p // 2 * count + i]
                o_ref[who, p % 2] = jnp.dot(
                    ref[i, nocc:], hold[2 * who + p % 2], preferred_element_type=F32
                ).astype(BF16)
                return carry

            lax.fori_loop(0, count, one, 0, unroll=2)
        for b in range(blocks):
            keep(b).wait()


def field_apply(owner, fields, pieces, cholesky):
    vectors, walkers = fields.shape
    m = cholesky.shape[1]
    flat = [p for pair in pieces for p in pair]
    nocc = flat[0].shape[1] // 2
    rows_p = 64
    vmem = pl.BlockSpec(memory_space=pltpu.VMEM)
    return pl.pallas_call(
        field_kernel,
        grid=(m // rows_p,),
        in_specs=[
            pl.BlockSpec(memory_space=pltpu.SMEM),
            vmem,
            pl.BlockSpec((vectors, rows_p, m), lambda i: (0, i, 0)),
        ]
        + [vmem] * len(flat),
        out_specs=[pl.BlockSpec(memory_space=pl.ANY), vmem],
        out_shape=[
            jax.ShapeDtypeStruct((walkers, m, m), BF16),
            jax.ShapeDtypeStruct((walkers // 2, 2, nocc, m), BF16),
        ],
        scratch_shapes=[
            pltpu.VMEM((walkers * 8, vectors * 8), BF16),
            pltpu.VMEM((walkers, m, m), BF16),
            pltpu.SemaphoreType.DMA((16,)),
        ],
        compiler_params=pltpu.CompilerParams(vmem_limit_bytes=58 << 20),
        cost_estimate=pl.CostEstimate(flops=18 << 30, bytes_accessed=54 << 20, transcendentals=0),
        name="field_apply",
    )(owner, fields, cholesky, *flat)


def apply_kernel(slot_ref, pa_ref, pb_ref, h_ref, x_ref, o_ref, hold, sems):
    nocc = pa_ref.shape[1]
    blocks = sems.shape[0]
    size = hold.shape[0] // blocks

    def fetch(b):
        at = pl.ds(b * size, size)
        return pltpu.make_async_copy(h_ref.at[at], hold.at[at], sems.at[b])

    for b in range(blocks):
        fetch(b).start()

    def one(b, carry):
        fetch(b).wait()
        for k in range(size // 2):
            i = b * (size // 2) + k
            x = pa_ref[slot_ref[0, i]]
            y = pb_ref[slot_ref[1, i]]
            o_ref[i, :nocc] = jnp.dot(x, hold[2 * i], preferred_element_type=F32).astype(BF16)
            o_ref[i, nocc : 2 * nocc] = jnp.dot(y, hold[2 * i + 1], preferred_element_type=F32).astype(BF16)
            o_ref[i, 2 * nocc :] = x_ref[i]
        return carry

    lax.fori_loop(0, blocks, one, 0)


def apply(table, pa, pb, h, extra):
    walkers, m, _ = h.shape
    nocc = pa.shape[1]
    vmem = pl.BlockSpec(memory_space=pltpu.VMEM)
    return pl.pallas_call(
        apply_kernel,
        in_specs=[pl.BlockSpec(memory_space=pltpu.SMEM), vmem, vmem, pl.BlockSpec(memory_space=pl.ANY), vmem],
        out_specs=vmem,
        out_shape=jax.ShapeDtypeStruct((walkers // 2, 2 * nocc + extra.shape[1], m), BF16),
        scratch_shapes=[pltpu.VMEM((walkers, m, m), BF16), pltpu.SemaphoreType.DMA((16,))],
        compiler_params=pltpu.CompilerParams(vmem_limit_bytes=58 << 20),
        cost_estimate=pl.CostEstimate(flops=6 << 30, bytes_accessed=40 << 20, transcendentals=0),
        name="apply",
    )(table, pa, pb, h, extra)


def exchange(a):
    return lax.all_to_all(a, "stretch", 0, 0, tiled=True)


def in_three(e):
    first = lax.reduce_precision(e, 8, 7)
    second = lax.reduce_precision(e - first, 8, 7)
    return jnp.stack([first, second, e - first - second], -1).astype(BF16)


def shards(walkers, inverse_intersection, half_rotated, cholesky, field_noise, branch_sources):
    count, nocc, m = walkers.shape
    group_size = count * S
    place = lax.axis_index("stretch")
    both = np.stack([slots(ORDER_A), slots(ORDER_B)], 1)
    owners = np.argsort(both, -1).astype(np.int32)
    table = lax.dynamic_index_in_dim(jnp.asarray(both), place, 0, keepdims=False)
    owner = lax.dynamic_index_in_dim(jnp.asarray(owners), place, 0, keepdims=False)
    green = jnp.einsum(
        "wij,wjp->wip", inverse_intersection, walkers, precision=lax.Precision.HIGHEST
    ).astype(BF16)
    pieces = gather_walkers(jnp.concatenate([green, walkers.astype(BF16)], 1))
    force_bias, fields, energy = intersect(owner, pieces, half_rotated, field_noise)
    h, part = field_apply(owner, fields, pieces, cholesky)
    first = jnp.sum(exchange(part).astype(F32), 0)
    pieces = gather_walkers(first.astype(BF16))
    qa, qb = (jnp.concatenate(p, 0) for p in zip(*pieces))
    extra = in_three(energy.reshape(S, count)).reshape(S, 1, count * 3)
    extra = jnp.pad(extra, ((0, 0), (0, 7), (0, m - count * 3)))
    part = apply(table, qa, qb, h, extra)
    got = jnp.sum(exchange(part).astype(F32), 0)
    second = got[: count * nocc].reshape(count, nocc, m) / 2
    exchange_energy = jnp.sum(got[count * nocc, : count * 3].reshape(count, 3), 1)
    propagated = walkers + first + second
    column = lax.all_gather(propagated, "walk", axis=0, tiled=True)
    position = branch_sources // group_size * count + branch_sources % count
    picked = jnp.take(column, position, axis=0)
    return (force_bias, exchange_energy, picked)


def solution(mesh):
    placed = (
        P(("walk", "stretch"), None, None),
        P(("walk", "stretch"), None, None),
        P("stretch", None, None),
        P("stretch", None, None),
        P("walk", "stretch"),
        P(("walk", "stretch")),
    )
    return jax.shard_map(
        shards,
        mesh=mesh,
        in_specs=placed,
        out_specs=(
            P("walk", "stretch"),
            P(("walk", "stretch")),
            P(("walk", "stretch"), None, None),
        ),
        check_vma=False,
    )
```

```python
import functools

import jax
import jax.numpy as jnp
import numpy as np
from jax import lax
from jax.experimental import pallas as pl
from jax.experimental.pallas import tpu as pltpu
from jax.sharding import PartitionSpec as P

ORDERS = 2
Z, Y, X = 4, 2, 4
S = Z * Y * X
STEP = {"z": (1, 0, 0), "y": (0, 1, 0), "x": (0, 0, 1)}
HEARD = (0, -1, 1, -2)
ORDER_A = "yxz"
ORDER_B = "yzx"
PAD = 64
WB = 8
F32 = jnp.float32
BF16 = jnp.bfloat16
NT = (((1,), (1,)), ((), ()))


def encode(z, y, x):
    return (z % Z) * (Y * X) + (y % Y) * X + (x % X)


def decode(s):
    return s // (Y * X), s // X % Y, s % X


def shift(a, axis, k):
    d = STEP[axis]
    pairs = []
    for s in range(S):
        z, y, x = decode(s)
        pairs.append((s, encode(z + d[0] * k, y + d[1] * k, x + d[2] * k)))
    return lax.ppermute(a, "stretch", pairs)


def around(a, axis):
    return [a, shift(a, axis, 1), shift(a, axis, -1), shift(a, axis, 2)]


def slots(order):
    table = np.zeros((S, S), np.int32)
    for s in range(S):
        offsets = [(0, 0, 0)]
        for axis in order:
            d = STEP[axis]
            heard = HEARD[:2] if axis == "y" else HEARD
            offsets = [tuple(o[i] + d[i] * h for i in range(3)) for h in heard for o in offsets]
        z, y, x = decode(s)
        for slot, o in enumerate(offsets):
            table[s, encode(z + o[0], y + o[1], x + o[2])] = slot
    return table


def gather_walkers(a):
    both = jnp.concatenate([a, shift(a, "y", 1)], 0)
    near = [jnp.concatenate(around(both[i::2], o[1]), 0) for i, o in enumerate((ORDER_A, ORDER_B))]
    far = [around(n, o[2]) for n, o in zip(near, (ORDER_A, ORDER_B))]
    return list(zip(*far))


def intersect_kernel(start, count, final, *refs):
    owner_ref, hr_ref = refs[:2]
    pieces = refs[2 : 2 + 2 * count]
    rest = refs[2 + 2 * count :]
    if start == 0:
        total, ht, hts, hp, hps = rest[:5]
    else:
        ht, hts = rest[:2]
        total = rest[2]
    if final:
        n_ref, *before, b_ref, f_ref, e_ref, total = rest[2 : 7 + start]
    he, ho, gp, gps, ge, go, sums = refs[-7:]
    step = pl.program_id(0)
    vectors, nocc = hr_ref.shape[:2]
    half = vectors // 2

    @pl.when(step == 0)
    def _():
        gp[...] = jnp.zeros_like(gp)
        gps[...] = jnp.zeros_like(gps)
        sums[...] = jnp.zeros_like(sums)
        total[...] = jnp.zeros_like(total)
        for g in range(half):
            for side, dense in ((0, he), (1, ho)):
                dense[g * nocc : (g + 1) * nocc, :] = hr_ref[side * half + g]
        if start == 0:
            hp[...] = jnp.zeros_like(hp)
            hps[...] = jnp.zeros_like(hps)
            for g in range(half):
                for side in range(2):
                    v = hr_ref[side * half + g]
                    at = (2 * g + side) * PAD
                    hp[at : at + nocc, :] = v
                    at = (2 * g + 1 - side) * PAD
                    hps[at : at + nocc, :] = v
            m = hp.shape[1]
            one = lax.broadcasted_iota(jnp.int32, (m, m), 0) == lax.broadcasted_iota(jnp.int32, (m, m), 1)
            unit = jnp.where(one, 1.0, 0.0).astype(BF16)
            for n in range(0, hp.shape[0], 512):
                cols = slice(n, n + 512)
                ht[:, cols] = lax.dot_general(unit, hp[cols, :], NT, preferred_element_type=F32).astype(BF16)
                hts[:, cols] = lax.dot_general(unit, hps[cols, :], NT, preferred_element_type=F32).astype(BF16)

    pairs = WB // 2
    held = pieces[0].shape[0]
    turns = held // pairs
    for q in range(count):

        @pl.when(step // turns == q)
        def _(q=q):
            for k in range(pairs):
                a = pieces[2 * q][step % turns * pairs + k, :nocc]
                b = pieces[2 * q + 1][step % turns * pairs + k, :nocc]
                gp[2 * k * PAD : 2 * k * PAD + nocc, :] = a
                gp[(2 * k + 1) * PAD : (2 * k + 1) * PAD + nocc, :] = b
                gps[(2 * k + 1) * PAD : (2 * k + 1) * PAD + nocc, :] = a
                gps[2 * k * PAD : 2 * k * PAD + nocc, :] = b
                ge[k * nocc : (k + 1) * nocc, :] = a
                go[k * nocc : (k + 1) * nocc, :] = b

    ae = lax.dot_general(he[...], gp[...], NT, preferred_element_type=F32)
    ao = lax.dot_general(ho[...], gps[...], NT, preferred_element_type=F32)
    be = jnp.dot(ge[...], ht[...], preferred_element_type=F32)
    bo = jnp.dot(go[...], hts[...], preferred_element_type=F32)
    lane = lax.broadcasted_iota(jnp.int32, (8, 128), 1)
    row = lax.broadcasted_iota(jnp.int32, (8, 128), 0)
    low = lane < PAD
    group = lane % PAD // 8
    diagonal = (lane % 8 == row) & (lane % PAD < nocc)
    for k in range(pairs):
        acc_e = jnp.zeros((8, 128), F32)
        acc_o = jnp.zeros((8, 128), F32)
        lw = slice(k * 128, k * 128 + 128)
        for g in range(half):
            de = do = None
            for t in range(nocc // 8):
                rg = slice(g * nocc + t * 8, g * nocc + t * 8 + 8)
                rw = slice(k * nocc + t * 8, k * nocc + t * 8 + 8)
                lg = slice(g * 128, g * 128 + 128)
                a0, a1 = ae[rg, lw], ao[rg, lw]
                c0, c1 = be[rw, lg], bo[rw, lg]
                acc_e += a0 * jnp.where(low, c0, c1)
                acc_o += a1 * jnp.where(low, c1, c0)
                de = a0 if t == 0 else jnp.where(group == t, a0, de)
                do = a1 if t == 0 else jnp.where(group == t, a1, do)
            sums[0, g : g + 1, lw] = jnp.sum(jnp.where(diagonal, de, 0.0), axis=0, keepdims=True)
            sums[1, g : g + 1, lw] = jnp.sum(jnp.where(diagonal, do, 0.0), axis=0, keepdims=True)
        sums[0, half : half + 1, lw] = jnp.sum(acc_e, axis=0, keepdims=True)
        sums[1, half : half + 1, lw] = jnp.sum(acc_o, axis=0, keepdims=True)
    walkers = total.shape[2]
    side = lax.broadcasted_iota(jnp.int32, (128, walkers), 0) // PAD
    target = lax.broadcasted_iota(jnp.int32, (128, walkers), 1)
    base = start * held + step * pairs
    for parity in range(2):
        picks = []
        for k in range(pairs):
            wa, wb = 2 * owner_ref[0, base + k], 2 * owner_ref[1, base + k] + 1
            walker = jnp.where(side == parity, wa, wb)
            picks.append(jnp.where(walker == target, 1.0, 0.0))
        pick = jnp.concatenate(picks, axis=0).astype(BF16)
        whole = sums[parity]
        first = whole.astype(BF16)
        rest = whole - first.astype(F32)
        second = rest.astype(BF16)
        third = (rest - second.astype(F32)).astype(BF16)
        acc = jnp.dot(first, pick, preferred_element_type=F32)
        acc += jnp.dot(second, pick, preferred_element_type=F32)
        acc += jnp.dot(third, pick, preferred_element_type=F32)
        total[parity] += acc

    if final:

        @pl.when(step == pl.num_programs(0) - 1)
        def _():
            whole = total[...]
            for other in before:
                whole += other[...]
            bias = 2.0 * jnp.concatenate([whole[0, :half], whole[1, :half]], axis=0)
            b_ref[...] = bias
            f_ref[...] = (0.05 * (n_ref[...] - bias)).astype(BF16)
            e_ref[...] = -0.5 * (whole[0, half:] + whole[1, half:])


def intersect(owner, pieces, half_rotated, noise):
    vectors, nocc, m = half_rotated.shape
    held = pieces[0][0].shape[0]
    walkers = 2 * held * len(pieces)
    vmem = pl.BlockSpec(memory_space=pltpu.VMEM)
    total = jax.ShapeDtypeStruct((2, vectors // 2 + 8, walkers), F32)
    turned = jax.ShapeDtypeStruct((m, vectors * PAD), BF16)
    before, both = [], []
    for start in range(len(pieces)):
        count, final = 1, start == len(pieces) - 1
        inputs = [owner, half_rotated, *pieces[start], *both] + ([noise.T, *before] if final else [])
        outs = [total, turned, turned] if start == 0 else [total]
        if final:
            outs = [
                jax.ShapeDtypeStruct((vectors, walkers), F32),
                jax.ShapeDtypeStruct((vectors, walkers), BF16),
                jax.ShapeDtypeStruct((8, walkers), F32),
                total,
            ]
        wide = [pltpu.VMEM((vectors * PAD, m), BF16)] * 2 if start == 0 else []
        got = pl.pallas_call(
            functools.partial(intersect_kernel, start, count, final),
            grid=(2 * held * count // WB,),
            in_specs=[pl.BlockSpec(memory_space=pltpu.SMEM)] + [vmem] * (len(inputs) - 1),
            out_specs=[vmem] * len(outs),
            out_shape=outs,
            scratch_shapes=wide
            + [
                pltpu.VMEM((vectors // 2 * nocc, m), BF16),
                pltpu.VMEM((vectors // 2 * nocc, m), BF16),
                pltpu.VMEM((WB * PAD, m), BF16),
                pltpu.VMEM((WB * PAD, m), BF16),
                pltpu.VMEM((WB // 2 * nocc, m), BF16),
                pltpu.VMEM((WB // 2 * nocc, m), BF16),
                pltpu.VMEM((2, vectors // 2 + 8, WB // 2 * 128), F32),
            ],
            compiler_params=pltpu.CompilerParams(vmem_limit_bytes=36 << 20),
            cost_estimate=pl.CostEstimate(
                flops=4 * vectors * nocc * 2 * held * count * PAD * m, bytes_accessed=4 << 20, transcendentals=0
            ),
            name=f"intersect_{start}",
        )(*inputs)
        before.append(got[0])
        if start == 0:
            both = got[1:]
    bias, fields, energy, _ = got
    return bias.T, fields, energy[0]


def field_kernel(owner_ref, f_ref, c_ref, *refs):
    *pieces, h_ref, o_ref, spread, hold, sems = refs
    step = pl.program_id(0)
    last = pl.num_programs(0) - 1
    vectors, walkers = f_ref.shape
    rows_p, m = c_ref.shape[1:]
    nocc = o_ref.shape[2]

    @pl.when(step == 0)
    def _():
        rows, cols = walkers * 8, vectors * 8
        r = lax.broadcasted_iota(jnp.int32, (rows, walkers), 0) // 8
        w = lax.broadcasted_iota(jnp.int32, (rows, walkers), 1)
        pick_w = jnp.where(r == w, 1.0, 0.0).astype(BF16)
        v = lax.broadcasted_iota(jnp.int32, (vectors, cols), 0)
        c = lax.broadcasted_iota(jnp.int32, (vectors, cols), 1) // 8
        pick_v = jnp.where(v == c, 1.0, 0.0).astype(BF16)
        wide = lax.dot_general(pick_w, f_ref[...], NT, preferred_element_type=F32).astype(BF16)
        wide = jnp.dot(wide, pick_v, preferred_element_type=F32)
        rr = lax.broadcasted_iota(jnp.int32, (rows, cols), 0) % 8
        cc = lax.broadcasted_iota(jnp.int32, (rows, cols), 1) % 8
        spread[...] = jnp.where(rr == cc, wide, 0.0).astype(BF16)

    for q in range(0, rows_p, 16):
        block = c_ref[:, q : q + 16, :].astype(F32)
        lo = block[:, :8, :].reshape(vectors * 8, m).astype(BF16)
        hi = block[:, 8:, :].reshape(vectors * 8, m).astype(BF16)
        hlo = jnp.dot(spread[...], lo, preferred_element_type=F32).reshape(walkers, 8, m)
        hhi = jnp.dot(spread[...], hi, preferred_element_type=F32).reshape(walkers, 8, m)
        at = pl.ds(pl.multiple_of(step * rows_p + q, 16), 16)
        hold[:, at, :] = jnp.concatenate([hlo, hhi], axis=1).astype(BF16)

    @pl.when(step == last)
    def _():
        blocks = sems.shape[0]
        size = walkers // blocks

        def keep(b):
            at = slice(b * size, (b + 1) * size)
            return pltpu.make_async_copy(hold.at[at], h_ref.at[at], sems.at[b])

        for b in range(blocks):
            keep(b).start()
        count = pieces[0].shape[0]
        for p, ref in enumerate(pieces):

            def one(i, carry, p=p, ref=ref):
                who = owner_ref[p % 2, p // 2 * count + i]
                o_ref[who, p % 2] = jnp.dot(
                    ref[i, nocc:], hold[2 * who + p % 2], preferred_element_type=F32
                ).astype(BF16)
                return carry

            lax.fori_loop(0, count, one, 0, unroll=2)
        for b in range(blocks):
            keep(b).wait()


def field_apply(owner, fields, pieces, cholesky):
    vectors, walkers = fields.shape
    m = cholesky.shape[1]
    flat = [p for pair in pieces for p in pair]
    nocc = flat[0].shape[1] // 2
    rows_p = 64
    vmem = pl.BlockSpec(memory_space=pltpu.VMEM)
    return pl.pallas_call(
        field_kernel,
        grid=(m // rows_p,),
        in_specs=[
            pl.BlockSpec(memory_space=pltpu.SMEM),
            vmem,
            pl.BlockSpec((vectors, rows_p, m), lambda i: (0, i, 0)),
        ]
        + [vmem] * len(flat),
        out_specs=[pl.BlockSpec(memory_space=pl.ANY), vmem],
        out_shape=[
            jax.ShapeDtypeStruct((walkers, m, m), BF16),
            jax.ShapeDtypeStruct((walkers // 2, 2, nocc, m), BF16),
        ],
        scratch_shapes=[
            pltpu.VMEM((walkers * 8, vectors * 8), BF16),
            pltpu.VMEM((walkers, m, m), BF16),
            pltpu.SemaphoreType.DMA((16,)),
        ],
        compiler_params=pltpu.CompilerParams(vmem_limit_bytes=58 << 20),
        cost_estimate=pl.CostEstimate(flops=18 << 30, bytes_accessed=54 << 20, transcendentals=0),
        name="field_apply",
    )(owner, fields, cholesky, *flat)


def apply_kernel(start, count, final, owner_ref, h_ref, *refs):
    pieces = refs[: 2 * count]
    hold, sems = refs[-2:]
    o_ref = refs[-3]
    held, nocc = pieces[0].shape[:2]
    first_slot = start * held

    def fetch(j):
        w = 2 * owner_ref[j % 2, first_slot + j // 2] + j % 2
        return pltpu.make_async_copy(h_ref.at[w], hold.at[j], sems.at[j])

    def begin(j, carry):
        fetch(j).start()
        return carry

    lax.fori_loop(0, 2 * held * count, begin, 0)

    def put(who, side, value):
        for n in range(4):
            at = n * 2 * nocc + side * nocc
            o_ref[who, at : at + nocc, :] = value[:, n * 128 : (n + 1) * 128]

    if final:
        e_ref, x_ref = refs[2 * count : 2 * count + 2]

        def old(i, carry):
            for side in range(2):
                put(owner_ref[side, i], side, e_ref[side, i])
            return carry

        lax.fori_loop(0, first_slot, old, 0)
        o_ref[:, 8 * nocc :, :] = x_ref[...]
    for q in range(count):

        def one(i, carry, q=q):
            for side in range(2):
                j = 2 * (q * held + i) + side
                fetch(j).wait()
                value = jnp.dot(pieces[2 * q + side][i], hold[j], preferred_element_type=F32).astype(BF16)
                if final:
                    put(owner_ref[side, first_slot + q * held + i], side, value)
                else:
                    o_ref[side, i] = value
            return carry

        lax.fori_loop(0, held, one, 0)


def apply(owner, pieces, h, extra):
    m = h.shape[1]
    held, nocc = pieces[0][0].shape[:2]
    vmem = pl.BlockSpec(memory_space=pltpu.VMEM)
    before = None
    for start, count in ((0, 1), (1, len(pieces) - 1)):
        final = start > 0
        flat = [p for pair in pieces[start : start + count] for p in pair]
        inputs = [*flat] + ([before, extra] if final else [])
        shape = (held * len(pieces), 8 * nocc + 8, 128) if final else (2, held, nocc, m)
        before = pl.pallas_call(
            functools.partial(apply_kernel, start, count, final),
            in_specs=[pl.BlockSpec(memory_space=pltpu.SMEM), pl.BlockSpec(memory_space=pl.ANY)] + [vmem] * len(inputs),
            out_specs=vmem,
            out_shape=jax.ShapeDtypeStruct(shape, BF16),
            scratch_shapes=[
                pltpu.VMEM((2 * held * count, m, m), BF16),
                pltpu.SemaphoreType.DMA((2 * held * count,)),
            ],
            compiler_params=pltpu.CompilerParams(vmem_limit_bytes=(22 if count == 1 else 44) << 20),
            cost_estimate=pl.CostEstimate(
                flops=count * (3 << 29), bytes_accessed=count * (10 << 20), transcendentals=0
            ),
            name=f"apply_{start}",
        )(owner, h, *inputs)
    return before


def exchange(a):
    return lax.all_to_all(a, "stretch", 0, 0, tiled=True)


def in_three(e):
    first = lax.reduce_precision(e, 8, 7)
    second = lax.reduce_precision(e - first, 8, 7)
    return jnp.stack([first, second, e - first - second], -1).astype(BF16)


def shards(walkers, inverse_intersection, half_rotated, cholesky, field_noise, branch_sources):
    count, nocc, m = walkers.shape
    group_size = count * S
    place = lax.axis_index("stretch")
    both = np.stack([slots(ORDER_A), slots(ORDER_B)], 1)
    owners = np.argsort(both, -1).astype(np.int32)
    owner = lax.dynamic_index_in_dim(jnp.asarray(owners), place, 0, keepdims=False)
    green = jnp.einsum(
        "wij,wjp->wip", inverse_intersection, walkers, precision=lax.Precision.HIGHEST
    ).astype(BF16)
    pieces = gather_walkers(jnp.concatenate([green, walkers.astype(BF16)], 1))
    force_bias, fields, energy = intersect(owner, pieces, half_rotated, field_noise)
    h, part = field_apply(owner, fields, pieces, cholesky)
    energy, part = lax.optimization_barrier((energy, part))
    first = jnp.sum(exchange(part).astype(F32), 0)
    pieces = gather_walkers(first.astype(BF16))
    extra = in_three(energy.reshape(S, count)).reshape(S, 1, count * 3)
    extra = jnp.pad(extra, ((0, 0), (0, 7), (0, 128 - count * 3)))
    part = apply(owner, pieces, h, extra)
    got = jnp.sum(exchange(part).astype(F32), 0)
    rows = 4 * count * nocc
    second = jnp.transpose(got[:rows].reshape(4, count, nocc, 128), (1, 2, 0, 3)).reshape(count, nocc, m) / 2
    exchange_energy = jnp.sum(got[rows, : count * 3].reshape(count, 3), 1)
    position = branch_sources // group_size * count + branch_sources % count
    column = lax.all_gather(walkers + first + second, "walk", axis=0, tiled=True)
    picked = jnp.take(column, position, axis=0)
    return (force_bias, exchange_energy, picked)


def solution(mesh):
    placed = (
        P(("walk", "stretch"), None, None),
        P(("walk", "stretch"), None, None),
        P("stretch", None, None),
        P("stretch", None, None),
        P("walk", "stretch"),
        P(("walk", "stretch")),
    )
    return jax.shard_map(
        shards,
        mesh=mesh,
        in_specs=placed,
        out_specs=(
            P("walk", "stretch"),
            P(("walk", "stretch")),
            P(("walk", "stretch"), None, None),
        ),
        check_vma=False,
    )
```

```python
import functools

import jax
import jax.numpy as jnp
import numpy as np
from jax import lax
from jax.experimental import pallas as pl
from jax.experimental.pallas import tpu as pltpu
from jax.sharding import PartitionSpec as P

ORDERS = 2
Z, Y, X = 4, 2, 4
S = Z * Y * X
STEP = {"z": (1, 0, 0), "y": (0, 1, 0), "x": (0, 0, 1)}
HEARD = (0, -1, 1, -2)
ORDER_A = "yxz"
ORDER_B = "yzx"
PAD = 64
WB = 8
F32 = jnp.float32
BF16 = jnp.bfloat16
NT = (((1,), (1,)), ((), ()))


def encode(z, y, x):
    return (z % Z) * (Y * X) + (y % Y) * X + (x % X)


def decode(s):
    return s // (Y * X), s // X % Y, s % X


def shift(a, axis, k):
    d = STEP[axis]
    pairs = []
    for s in range(S):
        z, y, x = decode(s)
        pairs.append((s, encode(z + d[0] * k, y + d[1] * k, x + d[2] * k)))
    return lax.ppermute(a, "stretch", pairs)


def around(a, axis):
    return [a, shift(a, axis, 1), shift(a, axis, -1), shift(a, axis, 2)]


def slots(order):
    table = np.zeros((S, S), np.int32)
    for s in range(S):
        offsets = [(0, 0, 0)]
        for axis in order:
            d = STEP[axis]
            heard = HEARD[:2] if axis == "y" else HEARD
            offsets = [tuple(o[i] + d[i] * h for i in range(3)) for h in heard for o in offsets]
        z, y, x = decode(s)
        for slot, o in enumerate(offsets):
            table[s, encode(z + o[0], y + o[1], x + o[2])] = slot
    return table


def gather_walkers(a):
    both = jnp.concatenate([a, shift(a, "y", 1)], 0)
    near = [jnp.concatenate(around(both[i::2], o[1]), 0) for i, o in enumerate((ORDER_A, ORDER_B))]
    far = [around(n, o[2]) for n, o in zip(near, (ORDER_A, ORDER_B))]
    return list(zip(*far))


def intersect_kernel(start, count, final, *refs):
    owner_ref, hr_ref = refs[:2]
    pieces = refs[2 : 2 + 2 * count]
    rest = refs[2 + 2 * count :]
    if start == 0:
        total, ht, hts, hp, hps = rest[:5]
    else:
        ht, hts = rest[:2]
        total = rest[2]
    if final:
        n_ref, *before, b_ref, f_ref, e_ref, total = rest[2 : 7 + start]
    gp, gps, ge, go, sums = refs[-5:]
    step = pl.program_id(0)
    vectors, nocc = hr_ref.shape[:2]
    half = vectors // 2

    @pl.when(step == 0)
    def _():
        gp[...] = jnp.zeros_like(gp)
        gps[...] = jnp.zeros_like(gps)
        sums[...] = jnp.zeros_like(sums)
        total[...] = jnp.zeros_like(total)
        if start == 0:
            hp[...] = jnp.zeros_like(hp)
            hps[...] = jnp.zeros_like(hps)
            for g in range(half):
                for side in range(2):
                    v = hr_ref[side * half + g]
                    at = (2 * g + side) * PAD
                    hp[at : at + nocc, :] = v
                    at = (2 * g + 1 - side) * PAD
                    hps[at : at + nocc, :] = v
            m = hp.shape[1]
            one = lax.broadcasted_iota(jnp.int32, (m, m), 0) == lax.broadcasted_iota(jnp.int32, (m, m), 1)
            unit = jnp.where(one, 1.0, 0.0).astype(BF16)
            for n in range(0, hp.shape[0], 512):
                cols = slice(n, n + 512)
                ht[:, cols] = lax.dot_general(unit, hp[cols, :], NT, preferred_element_type=F32).astype(BF16)
                hts[:, cols] = lax.dot_general(unit, hps[cols, :], NT, preferred_element_type=F32).astype(BF16)

    pairs = WB // 2
    held = pieces[0].shape[0]
    turns = held // pairs
    for q in range(count):

        @pl.when(step // turns == q)
        def _(q=q):
            for k in range(pairs):
                a = pieces[2 * q][step % turns * pairs + k, :nocc]
                b = pieces[2 * q + 1][step % turns * pairs + k, :nocc]
                gp[2 * k * PAD : 2 * k * PAD + nocc, :] = a
                gp[(2 * k + 1) * PAD : (2 * k + 1) * PAD + nocc, :] = b
                gps[(2 * k + 1) * PAD : (2 * k + 1) * PAD + nocc, :] = a
                gps[2 * k * PAD : 2 * k * PAD + nocc, :] = b
                ge[k * nocc : (k + 1) * nocc, :] = a
                go[k * nocc : (k + 1) * nocc, :] = b

    he = hr_ref[:half].reshape(half * nocc, hr_ref.shape[2])
    ho = hr_ref[half:].reshape(half * nocc, hr_ref.shape[2])
    ae = lax.dot_general(he, gp[...], NT, preferred_element_type=F32)
    ao = lax.dot_general(ho, gps[...], NT, preferred_element_type=F32)
    be = jnp.dot(ge[...], ht[...], preferred_element_type=F32)
    bo = jnp.dot(go[...], hts[...], preferred_element_type=F32)
    lane = lax.broadcasted_iota(jnp.int32, (8, 128), 1)
    row = lax.broadcasted_iota(jnp.int32, (8, 128), 0)
    low = lane < PAD
    group = lane % PAD // 8
    diagonal = (lane % 8 == row) & (lane % PAD < nocc)
    for k in range(pairs):
        acc_e = jnp.zeros((8, 128), F32)
        acc_o = jnp.zeros((8, 128), F32)
        lw = slice(k * 128, k * 128 + 128)
        for g in range(half):
            de = do = None
            for t in range(nocc // 8):
                rg = slice(g * nocc + t * 8, g * nocc + t * 8 + 8)
                rw = slice(k * nocc + t * 8, k * nocc + t * 8 + 8)
                lg = slice(g * 128, g * 128 + 128)
                a0, a1 = ae[rg, lw], ao[rg, lw]
                c0, c1 = be[rw, lg], bo[rw, lg]
                acc_e += a0 * jnp.where(low, c0, c1)
                acc_o += a1 * jnp.where(low, c1, c0)
                de = a0 if t == 0 else jnp.where(group == t, a0, de)
                do = a1 if t == 0 else jnp.where(group == t, a1, do)
            sums[0, g : g + 1, lw] = jnp.sum(jnp.where(diagonal, de, 0.0), axis=0, keepdims=True)
            sums[1, g : g + 1, lw] = jnp.sum(jnp.where(diagonal, do, 0.0), axis=0, keepdims=True)
        sums[0, half : half + 1, lw] = jnp.sum(acc_e, axis=0, keepdims=True)
        sums[1, half : half + 1, lw] = jnp.sum(acc_o, axis=0, keepdims=True)
    walkers = total.shape[2]
    side = lax.broadcasted_iota(jnp.int32, (128, walkers), 0) // PAD
    target = lax.broadcasted_iota(jnp.int32, (128, walkers), 1)
    base = start * held + step * pairs
    for parity in range(2):
        picks = []
        for k in range(pairs):
            wa, wb = 2 * owner_ref[0, base + k], 2 * owner_ref[1, base + k] + 1
            walker = jnp.where(side == parity, wa, wb)
            picks.append(jnp.where(walker == target, 1.0, 0.0))
        pick = jnp.concatenate(picks, axis=0).astype(BF16)
        whole = sums[parity]
        first = whole.astype(BF16)
        rest = whole - first.astype(F32)
        second = rest.astype(BF16)
        third = (rest - second.astype(F32)).astype(BF16)
        acc = jnp.dot(first, pick, preferred_element_type=F32)
        acc += jnp.dot(second, pick, preferred_element_type=F32)
        acc += jnp.dot(third, pick, preferred_element_type=F32)
        total[parity] += acc

    if final:

        @pl.when(step == pl.num_programs(0) - 1)
        def _():
            whole = total[...]
            for other in before:
                whole += other[...]
            bias = 2.0 * jnp.concatenate([whole[0, :half], whole[1, :half]], axis=0)
            b_ref[...] = bias
            f_ref[...] = (0.05 * (n_ref[...] - bias)).astype(BF16)
            e_ref[...] = -0.5 * (whole[0, half:] + whole[1, half:])


def intersect(owner, pieces, half_rotated, noise):
    vectors, nocc, m = half_rotated.shape
    held = pieces[0][0].shape[0]
    walkers = 2 * held * len(pieces)
    vmem = pl.BlockSpec(memory_space=pltpu.VMEM)
    total = jax.ShapeDtypeStruct((2, vectors // 2 + 8, walkers), F32)
    turned = jax.ShapeDtypeStruct((m, vectors * PAD), BF16)
    before, both = [], []
    for start in range(len(pieces)):
        count, final = 1, start == len(pieces) - 1
        inputs = [owner, half_rotated, *pieces[start], *both] + ([noise.T, *before] if final else [])
        outs = [total, turned, turned] if start == 0 else [total]
        if final:
            outs = [
                jax.ShapeDtypeStruct((vectors, walkers), F32),
                jax.ShapeDtypeStruct((vectors, walkers), BF16),
                jax.ShapeDtypeStruct((8, walkers), F32),
                total,
            ]
        wide = [pltpu.VMEM((vectors * PAD, m), BF16)] * 2 if start == 0 else []
        got = pl.pallas_call(
            functools.partial(intersect_kernel, start, count, final),
            grid=(2 * held * count // WB,),
            in_specs=[pl.BlockSpec(memory_space=pltpu.SMEM)] + [vmem] * (len(inputs) - 1),
            out_specs=[vmem] * len(outs),
            out_shape=outs,
            scratch_shapes=wide
            + [
                pltpu.VMEM((WB * PAD, m), BF16),
                pltpu.VMEM((WB * PAD, m), BF16),
                pltpu.VMEM((WB // 2 * nocc, m), BF16),
                pltpu.VMEM((WB // 2 * nocc, m), BF16),
                pltpu.VMEM((2, vectors // 2 + 8, WB // 2 * 128), F32),
            ],
            compiler_params=pltpu.CompilerParams(vmem_limit_bytes=36 << 20),
            cost_estimate=pl.CostEstimate(
                flops=4 * vectors * nocc * 2 * held * count * PAD * m, bytes_accessed=4 << 20, transcendentals=0
            ),
            name=f"intersect_{start}",
        )(*inputs)
        before.append(got[0])
        if start == 0:
            both = got[1:]
    bias, fields, energy, _ = got
    return bias.T, fields, energy[0]


def field_kernel(owner_ref, f_ref, c_ref, *refs):
    *pieces, h_ref, o_ref, spread, hold, sems = refs
    step = pl.program_id(0)
    last = pl.num_programs(0) - 1
    vectors, walkers = f_ref.shape
    rows_p, m = c_ref.shape[1:]
    nocc = o_ref.shape[2]

    @pl.when(step == 0)
    def _():
        rows, cols = walkers * 8, vectors * 8
        r = lax.broadcasted_iota(jnp.int32, (rows, walkers), 0) // 8
        w = lax.broadcasted_iota(jnp.int32, (rows, walkers), 1)
        pick_w = jnp.where(r == w, 1.0, 0.0).astype(BF16)
        v = lax.broadcasted_iota(jnp.int32, (vectors, cols), 0)
        c = lax.broadcasted_iota(jnp.int32, (vectors, cols), 1) // 8
        pick_v = jnp.where(v == c, 1.0, 0.0).astype(BF16)
        wide = lax.dot_general(pick_w, f_ref[...], NT, preferred_element_type=F32).astype(BF16)
        wide = jnp.dot(wide, pick_v, preferred_element_type=F32)
        rr = lax.broadcasted_iota(jnp.int32, (rows, cols), 0) % 8
        cc = lax.broadcasted_iota(jnp.int32, (rows, cols), 1) % 8
        spread[...] = jnp.where(rr == cc, wide, 0.0).astype(BF16)

    for q in range(0, rows_p, 16):
        block = c_ref[:, q : q + 16, :].astype(F32)
        lo = block[:, :8, :].reshape(vectors * 8, m).astype(BF16)
        hi = block[:, 8:, :].reshape(vectors * 8, m).astype(BF16)
        hlo = jnp.dot(spread[...], lo, preferred_element_type=F32).reshape(walkers, 8, m)
        hhi = jnp.dot(spread[...], hi, preferred_element_type=F32).reshape(walkers, 8, m)
        at = pl.ds(pl.multiple_of(step * rows_p + q, 16), 16)
        hold[:, at, :] = jnp.concatenate([hlo, hhi], axis=1).astype(BF16)

    @pl.when(step == last)
    def _():
        blocks = sems.shape[0]
        size = walkers // blocks

        def keep(b):
            at = slice(b * size, (b + 1) * size)
            return pltpu.make_async_copy(hold.at[at], h_ref.at[at], sems.at[b])

        for b in range(blocks):
            keep(b).start()
        count = pieces[0].shape[0]
        for p, ref in enumerate(pieces):

            def one(i, carry, p=p, ref=ref):
                who = owner_ref[p % 2, p // 2 * count + i]
                o_ref[who, p % 2] = jnp.dot(
                    ref[i, nocc:], hold[2 * who + p % 2], preferred_element_type=F32
                ).astype(BF16)
                return carry

            lax.fori_loop(0, count, one, 0, unroll=2)
        for b in range(blocks):
            keep(b).wait()


def field_apply(owner, fields, pieces, cholesky):
    vectors, walkers = fields.shape
    m = cholesky.shape[1]
    flat = [p for pair in pieces for p in pair]
    nocc = flat[0].shape[1] // 2
    rows_p = 64
    vmem = pl.BlockSpec(memory_space=pltpu.VMEM)
    return pl.pallas_call(
        field_kernel,
        grid=(m // rows_p,),
        in_specs=[
            pl.BlockSpec(memory_space=pltpu.SMEM),
            vmem,
            pl.BlockSpec((vectors, rows_p, m), lambda i: (0, i, 0)),
        ]
        + [vmem] * len(flat),
        out_specs=[pl.BlockSpec(memory_space=pl.ANY), vmem],
        out_shape=[
            jax.ShapeDtypeStruct((walkers, m, m), BF16),
            jax.ShapeDtypeStruct((walkers // 2, 2, nocc, m), BF16),
        ],
        scratch_shapes=[
            pltpu.VMEM((walkers * 8, vectors * 8), BF16),
            pltpu.VMEM((walkers, m, m), BF16),
            pltpu.SemaphoreType.DMA((16,)),
        ],
        compiler_params=pltpu.CompilerParams(vmem_limit_bytes=58 << 20),
        cost_estimate=pl.CostEstimate(flops=18 << 30, bytes_accessed=54 << 20, transcendentals=0),
        name="field_apply",
    )(owner, fields, cholesky, *flat)


def apply_kernel(start, count, final, owner_ref, h_ref, *refs):
    pieces = refs[: 2 * count]
    hold, sems = refs[-2:]
    o_ref = refs[-3]
    held, nocc = pieces[0].shape[:2]
    first_slot = start * held

    def fetch(j):
        w = 2 * owner_ref[j % 2, first_slot + j // 2] + j % 2
        return pltpu.make_async_copy(h_ref.at[w], hold.at[j], sems.at[j])

    def begin(j, carry):
        fetch(j).start()
        return carry

    lax.fori_loop(0, 2 * held * count, begin, 0)

    def put(who, side, value):
        for n in range(4):
            at = n * 2 * nocc + side * nocc
            o_ref[who, at : at + nocc, :] = value[:, n * 128 : (n + 1) * 128]

    if final:
        e_ref, x_ref = refs[2 * count : 2 * count + 2]

        def old(i, carry):
            for side in range(2):
                put(owner_ref[side, i], side, e_ref[side, i])
            return carry

        lax.fori_loop(0, first_slot, old, 0)
        o_ref[:, 8 * nocc :, :] = x_ref[...]
    for q in range(count):

        def one(i, carry, q=q):
            for side in range(2):
                j = 2 * (q * held + i) + side
                fetch(j).wait()
                value = jnp.dot(pieces[2 * q + side][i], hold[j], preferred_element_type=F32).astype(BF16)
                if final:
                    put(owner_ref[side, first_slot + q * held + i], side, value)
                else:
                    o_ref[side, i] = value
            return carry

        lax.fori_loop(0, held, one, 0)


def apply(owner, pieces, h, extra):
    m = h.shape[1]
    held, nocc = pieces[0][0].shape[:2]
    vmem = pl.BlockSpec(memory_space=pltpu.VMEM)
    before = None
    for start, count in ((0, 1), (1, len(pieces) - 1)):
        final = start > 0
        flat = [p for pair in pieces[start : start + count] for p in pair]
        inputs = [*flat] + ([before, extra] if final else [])
        shape = (held * len(pieces), 8 * nocc + 8, 128) if final else (2, held, nocc, m)
        before = pl.pallas_call(
            functools.partial(apply_kernel, start, count, final),
            in_specs=[pl.BlockSpec(memory_space=pltpu.SMEM), pl.BlockSpec(memory_space=pl.ANY)] + [vmem] * len(inputs),
            out_specs=vmem,
            out_shape=jax.ShapeDtypeStruct(shape, BF16),
            scratch_shapes=[
                pltpu.VMEM((2 * held * count, m, m), BF16),
                pltpu.SemaphoreType.DMA((2 * held * count,)),
            ],
            compiler_params=pltpu.CompilerParams(vmem_limit_bytes=(22 if count == 1 else 44) << 20),
            cost_estimate=pl.CostEstimate(
                flops=count * (3 << 29), bytes_accessed=count * (10 << 20), transcendentals=0
            ),
            name=f"apply_{start}",
        )(owner, h, *inputs)
    return before


def exchange(a):
    return lax.all_to_all(a, "stretch", 0, 0, tiled=True)


def in_three(e):
    first = lax.reduce_precision(e, 8, 7)
    second = lax.reduce_precision(e - first, 8, 7)
    return jnp.stack([first, second, e - first - second], -1).astype(BF16)


def shards(walkers, inverse_intersection, half_rotated, cholesky, field_noise, branch_sources):
    count, nocc, m = walkers.shape
    group_size = count * S
    place = lax.axis_index("stretch")
    both = np.stack([slots(ORDER_A), slots(ORDER_B)], 1)
    owners = np.argsort(both, -1).astype(np.int32)
    owner = lax.dynamic_index_in_dim(jnp.asarray(owners), place, 0, keepdims=False)
    green = jnp.einsum(
        "wij,wjp->wip", inverse_intersection, walkers, precision=lax.Precision.HIGHEST
    ).astype(BF16)
    pieces = gather_walkers(jnp.concatenate([green, walkers.astype(BF16)], 1))
    force_bias, fields, energy = intersect(owner, pieces, half_rotated, field_noise)
    h, part = field_apply(owner, fields, pieces, cholesky)
    energy, part = lax.optimization_barrier((energy, part))
    first = jnp.sum(exchange(part).astype(F32), 0)
    pieces = gather_walkers(first.astype(BF16))
    extra = in_three(energy.reshape(S, count)).reshape(S, 1, count * 3)
    extra = jnp.pad(extra, ((0, 0), (0, 7), (0, 128 - count * 3)))
    part = apply(owner, pieces, h, extra)
    got = jnp.sum(exchange(part).astype(F32), 0)
    rows = 4 * count * nocc
    second = jnp.transpose(got[:rows].reshape(4, count, nocc, 128), (1, 2, 0, 3)).reshape(count, nocc, m) / 2
    exchange_energy = jnp.sum(got[rows, : count * 3].reshape(count, 3), 1)
    position = branch_sources // group_size * count + branch_sources % count
    column = lax.all_gather(walkers + first + second, "walk", axis=0, tiled=True)
    picked = jnp.take(column, position, axis=0)
    return (force_bias, exchange_energy, picked)


def solution(mesh):
    placed = (
        P(("walk", "stretch"), None, None),
        P(("walk", "stretch"), None, None),
        P("stretch", None, None),
        P("stretch", None, None),
        P("walk", "stretch"),
        P(("walk", "stretch")),
    )
    return jax.shard_map(
        shards,
        mesh=mesh,
        in_specs=placed,
        out_specs=(
            P("walk", "stretch"),
            P(("walk", "stretch")),
            P(("walk", "stretch"), None, None),
        ),
        check_vma=False,
    )
```
